32 devices in a mesh: occ: 4 (over z), vir: 8 (over y, x, core).
Axes of the slice: x: 2, y: 2, z: 4, core: 2. Of those that a mesh axis runs over, the one named last changes fastest.
Arguments:
- amplitudes: float32 [64, 1441792], P(None, ('occ', 'vir')), may hold values from -6 to 6
- slab: float32 [128, 1441792], P(None, ('occ', 'vir')), may hold values from -0.0048828125 to 0.0048828125
- mirror: int32 [128], replicated, may hold values from 0 to 127, as said below
Outputs:
- ladder: float32 [64, 128], P('occ')
The draws below stay inside these ranges and needn't reach their ends.
Inputs may be any that keep to these rules, and one draw needn't show every extreme that they name: mirror pairs the rows: mirror[mirror[m]] = m and mirror[m] != m for every m.
All inputs are finite; a program needn't handle non-finite values.
Results may differ from the reference program's by a relative error of at most 0.000086.
Values sent between devices are 32-bit elements; how exact they have to be, the bound alone decides.
A program may use at most 128 MiB of HBM per device.

```python
import jax
import jax.numpy as jnp
from jax import lax

CD_PAIRS = 1441792
AB_PAIRS = 64
OCC_PAIRS = 64


def draw_mirror(key, part):
    count = 2 * AB_PAIRS
    order = jax.random.permutation(jax.random.fold_in(key, 17), count).astype(jnp.int32)
    first = order[0::2]
    second = order[1::2]
    paired = jnp.zeros((count,), jnp.int32).at[first].set(second).at[second].set(first)
    return paired


def strengthened(result, stream_key, source, target, blocks, factor):
    def block_of(position):
        return (jnp.arange(result.shape[position]) // (result.shape[position] // blocks)).reshape((-1,) + (1,) * (result.ndim - 1 - position))

    first = jax.random.permutation(stream_key, blocks)[block_of(target)]
    other_side = (block_of(target) + blocks // 2) % blocks
    return jnp.where((block_of(source) == first) | (block_of(source) == other_side), factor * result, result)


def shard_levels(key, extent, pieces, low, high):
    level = 1.0
    for dim, blocks in pieces:
        draws = jax.random.uniform(jax.random.fold_in(jax.random.fold_in(key, 6), dim), (blocks,), jnp.float32, low / len(pieces), high / len(pieces))
        level = level * jnp.repeat(jnp.exp(draws), extent[dim] // blocks).reshape((-1,) + (1,) * (len(extent) - 1 - dim))
    return level


def bell_draw(own_key, shape, scale, most, cuts=(), dtype=jnp.bfloat16):
    values = jax.random.normal(own_key, shape, jnp.float32) * scale
    if len(cuts) > 0:
        values = shard_levels(own_key, shape, cuts, -0.22, 0.18) * values
    return jnp.clip(values, min=-most, max=most).astype(dtype)


def bell_draw_with(own_key, extent, width, limit, split, heavy, kind=jnp.bfloat16):
    drawn = width * jax.random.normal(own_key, extent, jnp.float32)
    if split:
        drawn = drawn * shard_levels(own_key, extent, split, -0.22, 0.18)
    return jnp.clip(strengthened(drawn, jax.random.fold_in(own_key, 3), *heavy), -limit, limit).astype(kind)


def setup_inputs(seed: int = 0) -> dict:
    keys = jax.random.split(jax.random.key(seed), 4)
    amplitudes = bell_draw_with(keys[0], (OCC_PAIRS, CD_PAIRS), 1.0, 6.0, ((1, 32),), (1, 0, 32, 2.75), jnp.float32)
    slab = bell_draw(keys[1], (2 * AB_PAIRS, CD_PAIRS), CD_PAIRS ** -0.5, 0.0048828125, ((1, 32),), jnp.float32)
    mirror = draw_mirror(jax.random.fold_in(keys[3], 71), 0)
    return {"amplitudes": amplitudes, "slab": slab, "mirror": mirror}


def reference(amplitudes, slab, mirror):
    contracted = lax.dot_general(amplitudes, slab, (((1,), (1,)), ((), ())), precision=lax.Precision.HIGHEST, preferred_element_type=jnp.float32)
    return contracted - jnp.take(contracted, mirror, axis=1)
```

```python
import functools

import jax
import jax.numpy as jnp
from jax import lax
from jax.experimental import pallas as pl
from jax.experimental.pallas import tpu as pltpu
from jax.sharding import PartitionSpec as P

MESH = pl.DeviceIdType.MESH
LOOKAHEAD = 6
MOST_COLUMNS = 2816


def chunk_columns(depth):
    for columns in range(min(depth, MOST_COLUMNS) // 128 * 128, 0, -128):
        if depth % columns == 0:
            return columns
    return depth


def split(x):
    high = x.astype(jnp.bfloat16)
    low = (x - high.astype(jnp.float32)).astype(jnp.bfloat16)
    return jnp.concatenate([high, low], axis=0)


def kernel(n_occ, n_vir, columns, amp_hbm, slab_hbm, mirror_ref, out_ref, amp_buf, slab_buf, acc, part, by_occ, by_vir,
           amp_sem, slab_sem, occ_send, occ_recv, vir_send, vir_recv):
    occ, vir = lax.axis_index("occ"), lax.axis_index("vir")
    chunks = amp_buf.shape[0]
    rows, width = part.shape
    own_rows = rows // n_occ

    def copies(i):
        at = pl.ds(pl.multiple_of(i * columns, 128), columns)
        return (
            pltpu.make_async_copy(amp_hbm.at[:, at], amp_buf.at[i], amp_sem.at[i]),
            pltpu.make_async_copy(slab_hbm.at[:, at], slab_buf.at[i], slab_sem.at[i]),
        )

    ahead = min(LOOKAHEAD, chunks)
    for i in range(ahead):
        for copy in copies(i):
            copy.start()

    barrier = pltpu.get_barrier_semaphore()
    for d in range(1, n_occ):
        pl.semaphore_signal(barrier, inc=1, device_id=(lax.rem(occ + d, n_occ), vir), device_id_type=MESH)
    for d in range(1, n_vir):
        pl.semaphore_signal(barrier, inc=1, device_id=(occ, lax.rem(vir + d, n_vir)), device_id_type=MESH)

    acc[...] = jnp.zeros_like(acc)

    @pl.loop(0, chunks)
    def _(i):
        @pl.when(i + ahead < chunks)
        def _():
            for copy in copies(i + ahead):
                copy.start()

        for copy in copies(i):
            copy.wait()
        acc[...] += lax.dot_general(
            split(amp_buf[i]), split(slab_buf[i]), (((1,), (1,)), ((), ())), preferred_element_type=jnp.float32
        )

    part[...] = (acc[:rows, :width] + (acc[:rows, width:] + acc[rows:, :width])) + acc[rows:, width:]
    pl.semaphore_wait(barrier, n_occ + n_vir - 2)

    sends = []
    for d in range(1, n_occ):
        to = lax.rem(occ + d, n_occ)
        copy = pltpu.make_async_remote_copy(
            src_ref=part.at[pl.ds(pl.multiple_of(to * own_rows, 8), own_rows), :],
            dst_ref=by_occ.at[d - 1],
            send_sem=occ_send.at[d - 1],
            recv_sem=occ_recv.at[d - 1],
            device_id=(to, vir),
            device_id_type=MESH,
        )
        copy.start()
        sends.append(copy)
    total = part[pl.ds(pl.multiple_of(occ * own_rows, 8), own_rows), :]
    for d in range(1, n_occ):
        sends[d - 1].wait_recv()
        total = total + by_occ[d - 1]
    by_vir[vir] = total

    for d in range(1, n_vir):
        copy = pltpu.make_async_remote_copy(
            src_ref=by_vir.at[vir],
            dst_ref=by_vir.at[vir],
            send_sem=vir_send.at[d - 1],
            recv_sem=vir_recv.at[vir],
            device_id=(occ, lax.rem(vir + d, n_vir)),
            device_id_type=MESH,
        )
        copy.start()
        sends.append(copy)
    for d in range(1, n_vir):
        source = lax.rem(vir + d, n_vir)
        pltpu.make_async_remote_copy(
            src_ref=by_vir.at[source],
            dst_ref=by_vir.at[source],
            send_sem=vir_send.at[d - 1],
            recv_sem=vir_recv.at[source],
            device_id=(occ, source),
            device_id_type=MESH,
        ).wait_recv()
    total = by_vir[0]
    for source in range(1, n_vir):
        total = total + by_vir[source]
    index = jnp.broadcast_to(mirror_ref[...], total.shape)
    out_ref[...] = total - jnp.take_along_axis(total, index, axis=1)
    for copy in sends:
        copy.wait_send()


def per_device(amplitudes, slab, mirror):
    n_occ, n_vir = lax.axis_size("occ"), lax.axis_size("vir")
    rows, depth = amplitudes.shape
    width = slab.shape[0]
    own_rows = rows // n_occ
    columns = chunk_columns(depth)
    chunks = depth // columns
    return pl.pallas_call(
        functools.partial(kernel, n_occ, n_vir, columns),
        out_shape=jax.ShapeDtypeStruct((own_rows, width), jnp.float32),
        in_specs=[
            pl.BlockSpec(memory_space=pltpu.MemorySpace.HBM),
            pl.BlockSpec(memory_space=pltpu.MemorySpace.HBM),
            pl.BlockSpec(memory_space=pltpu.VMEM),
        ],
        out_specs=pl.BlockSpec(memory_space=pltpu.VMEM),
        scratch_shapes=[
            pltpu.VMEM((chunks, rows, columns), jnp.float32),
            pltpu.VMEM((chunks, width, columns), jnp.float32),
            pltpu.VMEM((2 * rows, 2 * width), jnp.float32),
            pltpu.VMEM((rows, width), jnp.float32),
            pltpu.VMEM((n_occ - 1, own_rows, width), jnp.float32),
            pltpu.VMEM((n_vir, own_rows, width), jnp.float32),
            pltpu.SemaphoreType.DMA((chunks,)),
            pltpu.SemaphoreType.DMA((chunks,)),
            pltpu.SemaphoreType.DMA((n_occ - 1,)),
            pltpu.SemaphoreType.DMA((n_occ - 1,)),
            pltpu.SemaphoreType.DMA((n_vir - 1,)),
            pltpu.SemaphoreType.DMA((n_vir,)),
        ],
        compiler_params=pltpu.CompilerParams(
            collective_id=0, has_side_effects=True, vmem_limit_bytes=60 * 2**20
        ),
    )(amplitudes, slab, mirror.reshape(1, width))


def solution(mesh):
    placed = (P(None, ("occ", "vir")), P(None, ("occ", "vir")), P())
    return jax.shard_map(
        per_device, mesh=mesh, in_specs=placed, out_specs=P("occ", None), check_vma=False
    )
```

```python
import functools

import jax
import jax.numpy as jnp
from jax import lax
from jax.experimental import pallas as pl
from jax.experimental.pallas import tpu as pltpu
from jax.sharding import PartitionSpec as P

MESH = pl.DeviceIdType.MESH
LOOKAHEAD = 6
MOST_COLUMNS = 2816


def chunk_columns(depth):
    for columns in range(min(depth, MOST_COLUMNS) // 128 * 128, 0, -128):
        if depth % columns == 0:
            return columns
    return depth


def split(x):
    high = x.astype(jnp.bfloat16)
    low = (x - high.astype(jnp.float32)).astype(jnp.bfloat16)
    return jnp.concatenate([high, low], axis=0)


def kernel(n_occ, n_vir, columns, amp_hbm, slab_hbm, mirror_hbm, out_ref, amp_buf, slab_buf, mirror_buf, acc, part, by_rank,
           by_vir, amp_sem, slab_sem, mirror_sem, rank_send, rank_recv, vir_send, vir_recv):
    occ, vir = lax.axis_index("occ"), lax.axis_index("vir")
    chunks = amp_buf.shape[0]
    rows, width = part.shape
    n_half = 2
    half_rows = rows // n_occ // n_half
    half = lax.rem(vir, n_half)
    pair = vir - half
    ranks = n_occ * n_half
    rank = occ * n_half + half

    def ranked(d):
        other = lax.rem(rank + d, ranks)
        return other, (other // n_half, pair + lax.rem(other, n_half))

    def copies(i):
        at = pl.ds(pl.multiple_of(i * columns, 128), columns)
        return (
            pltpu.make_async_copy(amp_hbm.at[:, at], amp_buf.at[i], amp_sem.at[i]),
            pltpu.make_async_copy(slab_hbm.at[:, at], slab_buf.at[i], slab_sem.at[i]),
        )

    ahead = min(LOOKAHEAD, chunks)
    for i in range(ahead):
        for copy in copies(i):
            copy.start()

    mirror_copy = pltpu.make_async_copy(mirror_hbm, mirror_buf, mirror_sem)
    mirror_copy.start()

    barrier = pltpu.get_barrier_semaphore()
    for d in range(1, ranks):
        pl.semaphore_signal(barrier, inc=1, device_id=ranked(d)[1], device_id_type=MESH)
    for d in range(n_half, n_vir):
        pl.semaphore_signal(barrier, inc=1, device_id=(occ, lax.rem(pair + d, n_vir)), device_id_type=MESH)

    acc[...] = jnp.zeros_like(acc)

    @pl.loop(0, chunks)
    def _(i):
        @pl.when(i + ahead < chunks)
        def _():
            for copy in copies(i + ahead):
                copy.start()

        for copy in copies(i):
            copy.wait()
        acc[...] += lax.dot_general(
            split(amp_buf[i]), split(slab_buf[i]), (((1,), (1,)), ((), ())), preferred_element_type=jnp.float32
        )

    part[...] = (acc[:rows, :width] + (acc[:rows, width:] + acc[rows:, :width])) + acc[rows:, width:]
    pl.semaphore_wait(barrier, ranks - 1 + n_vir - n_half)

    def rows_of(other):
        return part.at[pl.ds(pl.multiple_of(other * half_rows, 8), half_rows), :]

    sends = []
    for d in range(1, ranks):
        other, device = ranked(d)
        copy = pltpu.make_async_remote_copy(
            src_ref=rows_of(other),
            dst_ref=by_rank.at[d - 1],
            send_sem=rank_send.at[d - 1],
            recv_sem=rank_recv.at[d - 1],
            device_id=device,
            device_id_type=MESH,
        )
        copy.start()
        sends.append(copy)
    total = rows_of(rank)[...]
    for d in range(1, ranks):
        sends[d - 1].wait_recv()
        total = total + by_rank[d - 1]
    by_vir[vir] = total

    for d in range(1, n_vir):
        copy = pltpu.make_async_remote_copy(
            src_ref=by_vir.at[vir],
            dst_ref=by_vir.at[vir],
            send_sem=vir_send.at[d - 1],
            recv_sem=vir_recv.at[vir],
            device_id=(occ, lax.rem(vir + d, n_vir)),
            device_id_type=MESH,
        )
        copy.start()
        sends.append(copy)
    for d in range(1, n_vir):
        source = lax.rem(vir + d, n_vir)
        pltpu.make_async_remote_copy(
            src_ref=by_vir.at[source],
            dst_ref=by_vir.at[source],
            send_sem=vir_send.at[d - 1],
            recv_sem=vir_recv.at[source],
            device_id=(occ, source),
            device_id_type=MESH,
        ).wait_recv()
    mirror_copy.wait()
    for h in range(n_half):
        total = by_vir[h]
        for source in range(h + n_half, n_vir, n_half):
            total = total + by_vir[source]
        index = jnp.broadcast_to(mirror_buf[...], total.shape)
        out_ref[h * half_rows:(h + 1) * half_rows, :] = total - jnp.take_along_axis(total, index, axis=1)
    for copy in sends:
        copy.wait_send()


def per_device(amplitudes, slab, mirror):
    n_occ, n_vir = lax.axis_size("occ"), lax.axis_size("vir")
    rows, depth = amplitudes.shape
    width = slab.shape[0]
    own_rows = rows // n_occ
    columns = chunk_columns(depth)
    chunks = depth // columns
    return pl.pallas_call(
        functools.partial(kernel, n_occ, n_vir, columns),
        out_shape=pltpu.VMEM((own_rows, width), jnp.float32),
        in_specs=[
            pl.BlockSpec(memory_space=pltpu.MemorySpace.HBM),
            pl.BlockSpec(memory_space=pltpu.MemorySpace.HBM),
            pl.BlockSpec(memory_space=pltpu.MemorySpace.HBM),
        ],
        out_specs=pl.BlockSpec(memory_space=pltpu.VMEM),
        scratch_shapes=[
            pltpu.VMEM((chunks, rows, columns), jnp.float32),
            pltpu.VMEM((chunks, width, columns), jnp.float32),
            pltpu.VMEM((1, width), jnp.int32),
            pltpu.VMEM((2 * rows, 2 * width), jnp.float32),
            pltpu.VMEM((rows, width), jnp.float32),
            pltpu.VMEM((2 * n_occ - 1, own_rows // 2, width), jnp.float32),
            pltpu.VMEM((n_vir, own_rows // 2, width), jnp.float32),
            pltpu.SemaphoreType.DMA((chunks,)),
            pltpu.SemaphoreType.DMA((chunks,)),
            pltpu.SemaphoreType.DMA(()),
            pltpu.SemaphoreType.DMA((2 * n_occ - 1,)),
            pltpu.SemaphoreType.DMA((2 * n_occ - 1,)),
            pltpu.SemaphoreType.DMA((n_vir - 1,)),
            pltpu.SemaphoreType.DMA((n_vir,)),
        ],
        compiler_params=pltpu.CompilerParams(
            collective_id=0, has_side_effects=True, vmem_limit_bytes=60 * 2**20
        ),
    )(amplitudes, slab, mirror.reshape(1, width))


def solution(mesh):
    placed = (P(None, ("occ", "vir")), P(None, ("occ", "vir")), P())
    return jax.shard_map(
        per_device, mesh=mesh, in_specs=placed, out_specs=P("occ", None), check_vma=False
    )
```

```python
import functools

import jax
import jax.numpy as jnp
from jax import lax
from jax.experimental import pallas as pl
from jax.experimental.pallas import tpu as pltpu
from jax.sharding import PartitionSpec as P

MESH = pl.DeviceIdType.MESH
LOOKAHEAD = 4
MOST_COLUMNS = 4096


def chunk_columns(depth):
    for columns in range(min(depth, MOST_COLUMNS) // 128 * 128, 0, -128):
        if depth % columns == 0:
            return columns
    return depth


def split(x):
    high = x.astype(jnp.bfloat16)
    low = (x - high.astype(jnp.float32)).astype(jnp.bfloat16)
    return jnp.concatenate([high, low], axis=0)


def kernel(n_occ, n_vir, columns, amp_hbm, slab_hbm, mirror_hbm, out_ref, amp_buf, slab_buf, mirror_buf, acc, part, by_rank,
           by_vir, amp_sem, slab_sem, mirror_sem, rank_send, rank_recv, vir_send, vir_recv):
    occ, vir = lax.axis_index("occ"), lax.axis_index("vir")
    chunks = amp_buf.shape[0]
    rows, width = part.shape
    n_half = 2
    half_rows = rows // n_occ // n_half
    half = lax.rem(vir, n_half)
    pair = vir - half
    ranks = n_occ * n_half
    rank = occ * n_half + half

    def ranked(d):
        other = lax.rem(rank + d, ranks)
        return other, (other // n_half, pair + lax.rem(other, n_half))

    def copies(i):
        at = pl.ds(pl.multiple_of(i * columns, 128), columns)
        return (
            pltpu.make_async_copy(amp_hbm.at[:, at], amp_buf.at[i], amp_sem.at[i]),
            pltpu.make_async_copy(slab_hbm.at[:, at], slab_buf.at[i], slab_sem.at[i]),
        )

    ahead = min(LOOKAHEAD, chunks)
    for i in range(ahead):
        for copy in copies(i):
            copy.start()

    mirror_copy = pltpu.make_async_copy(mirror_hbm, mirror_buf, mirror_sem)
    mirror_copy.start()

    barrier = pltpu.get_barrier_semaphore()
    for d in range(1, ranks):
        pl.semaphore_signal(barrier, inc=1, device_id=ranked(d)[1], device_id_type=MESH)
    for d in range(n_half, n_vir):
        pl.semaphore_signal(barrier, inc=1, device_id=(occ, lax.rem(pair + d, n_vir)), device_id_type=MESH)

    acc[...] = jnp.zeros_like(acc)

    @pl.loop(0, chunks)
    def _(i):
        @pl.when(i + ahead < chunks)
        def _():
            for copy in copies(i + ahead):
                copy.start()

        for copy in copies(i):
            copy.wait()
        acc[...] += lax.dot_general(
            split(amp_buf[i]), split(slab_buf[i]), (((1,), (1,)), ((), ())), preferred_element_type=jnp.float32
        )

    part[...] = (acc[:rows, :width] + (acc[:rows, width:] + acc[rows:, :width])) + acc[rows:, width:]
    pl.semaphore_wait(barrier, ranks - 1 + n_vir - n_half)

    def rows_of(other):
        return part.at[pl.ds(pl.multiple_of(other * half_rows, 8), half_rows), :]

    sends = []
    for d in range(1, ranks):
        other, device = ranked(d)
        copy = pltpu.make_async_remote_copy(
            src_ref=rows_of(other),
            dst_ref=by_rank.at[d - 1],
            send_sem=rank_send.at[d - 1],
            recv_sem=rank_recv.at[d - 1],
            device_id=device,
            device_id_type=MESH,
        )
        copy.start()
        sends.append(copy)
    total = rows_of(rank)[...]
    for d in range(1, ranks):
        sends[d - 1].wait_recv()
        total = total + by_rank[d - 1]
    by_vir[vir] = total

    for d in range(1, n_vir):
        copy = pltpu.make_async_remote_copy(
            src_ref=by_vir.at[vir],
            dst_ref=by_vir.at[vir],
            send_sem=vir_send.at[d - 1],
            recv_sem=vir_recv.at[vir],
            device_id=(occ, lax.rem(vir + d, n_vir)),
            device_id_type=MESH,
        )
        copy.start()
        sends.append(copy)
    for d in range(1, n_vir):
        source = lax.rem(vir + d, n_vir)
        pltpu.make_async_remote_copy(
            src_ref=by_vir.at[source],
            dst_ref=by_vir.at[source],
            send_sem=vir_send.at[d - 1],
            recv_sem=vir_recv.at[source],
            device_id=(occ, source),
            device_id_type=MESH,
        ).wait_recv()
    mirror_copy.wait()
    for h in range(n_half):
        total = by_vir[h]
        for source in range(h + n_half, n_vir, n_half):
            total = total + by_vir[source]
        index = jnp.broadcast_to(mirror_buf[...], total.shape)
        out_ref[h * half_rows:(h + 1) * half_rows, :] = total - jnp.take_along_axis(total, index, axis=1)
    for copy in sends:
        copy.wait_send()


def per_device(amplitudes, slab, mirror):
    n_occ, n_vir = lax.axis_size("occ"), lax.axis_size("vir")
    rows, depth = amplitudes.shape
    width = slab.shape[0]
    own_rows = rows // n_occ
    columns = chunk_columns(depth)
    chunks = depth // columns
    return pl.pallas_call(
        functools.partial(kernel, n_occ, n_vir, columns),
        out_shape=pltpu.VMEM((own_rows, width), jnp.float32),
        in_specs=[
            pl.BlockSpec(memory_space=pltpu.MemorySpace.HBM),
            pl.BlockSpec(memory_space=pltpu.MemorySpace.HBM),
            pl.BlockSpec(memory_space=pltpu.MemorySpace.HBM),
        ],
        out_specs=pl.BlockSpec(memory_space=pltpu.VMEM),
        scratch_shapes=[
            pltpu.VMEM((chunks, rows, columns), jnp.float32),
            pltpu.VMEM((chunks, width, columns), jnp.float32),
            pltpu.VMEM((1, width), jnp.int32),
            pltpu.VMEM((2 * rows, 2 * width), jnp.float32),
            pltpu.VMEM((rows, width), jnp.float32),
            pltpu.VMEM((2 * n_occ - 1, own_rows // 2, width), jnp.float32),
            pltpu.VMEM((n_vir, own_rows // 2, width), jnp.float32),
            pltpu.SemaphoreType.DMA((chunks,)),
            pltpu.SemaphoreType.DMA((chunks,)),
            pltpu.SemaphoreType.DMA(()),
            pltpu.SemaphoreType.DMA((2 * n_occ - 1,)),
            pltpu.SemaphoreType.DMA((2 * n_occ - 1,)),
            pltpu.SemaphoreType.DMA((n_vir - 1,)),
            pltpu.SemaphoreType.DMA((n_vir,)),
        ],
        compiler_params=pltpu.CompilerParams(
            collective_id=0, has_side_effects=True, vmem_limit_bytes=60 * 2**20
        ),
    )(amplitudes, slab, mirror.reshape(1, width))


def solution(mesh):
    placed = (P(None, ("occ", "vir")), P(None, ("occ", "vir")), P())
    return jax.shard_map(
        per_device, mesh=mesh, in_specs=placed, out_specs=P("occ", None), check_vma=False
    )
```
